32 devices in a mesh: dom: 8 (over z, y), feat: 4 (over x, core).
Axes of the slice: x: 2, y: 2, z: 4, core: 2. Of those that a mesh axis runs over, the one named last changes fastest.
Arguments:
- feats: bfloat16 [16384, 1024], P('dom', 'feat'), may hold values from -6 to 6
- projection: bfloat16 [1024, 512], P('feat'), may hold values from -0.1875 to 0.1875
- tiles: bfloat16 [1024, 4, 128, 128], P(('dom', 'feat')), may hold values from -0.25 to 0.25
- slot_owner: int32 [1024, 1], P(('dom', 'feat')), may hold values from 0 to 7; in each aligned block of 32 rows (0 to 31, 32 to 63, ...) at most 8 rows name the same one
- slot_block: int32 [1024, 1], P(('dom', 'feat')), may hold values from 0 to 3
- source_block: int32 [1024, 4], P(('dom', 'feat')), may hold values from 0 to 3
- counts: int32 [16384], P(('dom', 'feat')), may hold values from 1 to 4
- out_grad: bfloat16 [16384, 256], P(('dom', 'feat')), may hold values from -0.046875 to 0.046875
Outputs:
- activated: bfloat16 [16384, 256], P(('dom', 'feat'))
- weight_grad: float32 [1024, 512], P('feat')
The draws below stay inside these ranges and needn't reach their ends.
Inputs may be any that keep to these rules, and one draw needn't show every extreme that they name: `slot_owner`: among the 32 sent rows of one device, no dom index is named more than 8 times; some device names one exactly 8 times.
All inputs are finite; a program needn't handle non-finite values.
Results may differ from the reference program's by a relative error of at most 0.0059.
Values may be sent and summed in bfloat16 or wider, within the bound.
No kernel may reach another device: no remote copies, remote signals or barrier semaphores. Data moves between devices by JAX's collectives and lax.ppermute only.
A program may use at most 128 MiB of HBM per device.

```python
import math
import jax
import jax.numpy as jnp
import numpy as np
from jax import lax

F = 1024
HID = 256
BLOCK = 128
BLK_DEV = 4
SLOTS_DEV = 32
KB = 4
CAP = 8
NODES = 16384
SLOTS = 1024
N_DOM = 8
N_FEAT = 4


def touch_ends(entries, key, low, high):
    spot = [jax.random.randint(jax.random.fold_in(key, axis), (), 0, length) for axis, length in enumerate(entries.shape)]
    longest = entries.shape.index(max(entries.shape))
    beside = spot[:longest] + [(spot[longest] + 1) % entries.shape[longest]] + spot[longest + 1:]
    return entries.at[tuple(spot)].set(low).at[tuple(beside)].set(high)


def level_of(rng, shape, cuts, least, largest):
    loudness, own = 1.0, jax.random.fold_in(rng, 6)
    for dim, parts in cuts:
        draws = jnp.exp(jax.random.uniform(jax.random.fold_in(own, dim), (parts,), jnp.float32, least / len(cuts), largest / len(cuts)))
        loudness = loudness * jnp.repeat(draws, shape[dim] // parts).reshape([-1 if axis == dim else 1 for axis in range(len(shape))])
    return loudness


def assign_block(rng, own, number, rows, count, top, most, skew):
    sequence = jax.random.permutation(rng, count)
    crowded, common = shares(count, rows * top, most, skew, True), shares(count, rows * top, most, skew, False)
    places = jnp.arange(count)

    def named(tallies, turn):
        used = int((tallies > 0).sum())
        fixed = max(1, used // 4)
        passed = fixed + (places - fixed + turn * (used - fixed)) % max(1, count - fixed)
        return jnp.zeros((count,), jnp.int32).at[sequence[jnp.where(places < fixed, places, passed)]].set(jnp.asarray(tallies, jnp.int32))

    tallies = jnp.where(number % 4 == 0, named(crowded, number // 4), named(common, number - number // 4 - 1))
    mixed = jax.random.permutation(jax.random.fold_in(own, 3), count)
    donor, sink = mixed[0:count // 2 * 2:2], mixed[1:count // 2 * 2:2]
    slack = jnp.minimum(tallies[donor] - 1, most - tallies[sink]) // 2
    slack = jnp.where((donor == sequence[0]) | (sink == sequence[0]) | (tallies[sink] == 0), 0, jnp.maximum(slack, 0))
    passed = jax.random.randint(jax.random.fold_in(own, 4), (count // 2,), 0, 1 << 20) % (slack + 1)
    tallies = tallies.at[donor].add(-passed).at[sink].add(passed)
    labels = jnp.searchsorted(jnp.cumsum(tallies), jnp.arange(rows * top), side="right").astype(jnp.int32)
    grid = labels.reshape(top, rows).T
    grid = grid[jax.random.permutation(jax.random.fold_in(own, 1), rows)]
    turn = jax.random.randint(jax.random.fold_in(own, 2), (rows, 1), 0, top)
    return jnp.take_along_axis(grid, (jnp.arange(top)[None, :] + turn) % top, axis=1)


def shares(amount, total, bound, skew, full):
    portions = [(1 << 20) // math.isqrt(grade ** skew) + 1 for grade in range(1, amount + 1)]
    largest = bound if full else min(bound, max(-(-total // amount), total * portions[0] // sum(portions)))
    least = 1 if total - largest >= amount - 1 else 0
    given, spare = [largest] + [least] * (amount - 1), total - largest - least * (amount - 1)
    while spare > 0:
        movable = [i for i in range(1, amount) if given[i] < largest] or [i for i in range(1, amount) if given[i] < bound]
        pool, left = sum([portions[i] for i in movable]), spare
        for i in movable:
            extra = min(bound - given[i], max(1, left * portions[i] // pool), spare)
            given[i] = given[i] + extra
            spare = spare - extra
    return np.array(given)


def centred(rng, extent, deviation, reach, split=(), held_as=jnp.bfloat16):
    result = deviation * jax.random.normal(rng, extent, jnp.float32)
    if split:
        result = result * level_of(rng, extent, split, -0.22, 0.18)
    return jnp.clip(result, -reach, reach).astype(held_as)


def setup_inputs(seed: int = 0) -> dict:
    key_of = jax.random.split(jax.random.key(seed), 9)
    feats = centred(key_of[0], (NODES, F), 1.0, 6.0, ((0, 8), (1, 4)))
    projection = centred(key_of[1], (F, 2 * HID), F ** -0.5, 0.1875, ((0, 4),))
    tiles = centred(key_of[2], (SLOTS, KB, BLOCK, BLOCK), (KB * BLOCK) ** -0.5, 0.25, ((0, 32),))
    slot_owner_keys = jax.random.split(jax.random.fold_in(key_of[3], 1), SLOTS // SLOTS_DEV)
    slot_owner_turns = jax.random.permutation(jax.random.fold_in(key_of[3], 3), SLOTS // SLOTS_DEV)
    slot_owner = jax.vmap(lambda own, number: assign_block(jax.random.fold_in(key_of[3], 2), own, number, SLOTS_DEV, N_DOM, 1, CAP, 2))(slot_owner_keys, slot_owner_turns).reshape((SLOTS, 1))
    slot_block = touch_ends(jax.random.randint(key_of[4], (SLOTS, 1), 0, BLK_DEV), jax.random.fold_in(key_of[4], 1), 0, BLK_DEV - 1).astype(jnp.int32)
    source_block = touch_ends(jax.random.randint(key_of[5], (SLOTS, KB), 0, BLK_DEV), jax.random.fold_in(key_of[5], 1), 0, BLK_DEV - 1).astype(jnp.int32)
    counts = touch_ends(jax.random.randint(key_of[6], (NODES,), 1, 5), jax.random.fold_in(key_of[6], 1), 1, 4).astype(jnp.int32)
    out_grad = centred(key_of[7], (NODES, HID), NODES ** -0.5, 0.046875, ((0, 32),))
    return dict(feats=feats, projection=projection, tiles=tiles, slot_owner=slot_owner, slot_block=slot_block, source_block=source_block, counts=counts, out_grad=out_grad)


def reference(feats, projection, tiles, slot_owner, slot_block, source_block, counts, out_grad):
    tile_size = tiles.shape[-1]
    out_width = out_grad.shape[1]
    devices = N_DOM * N_FEAT
    projected = jnp.dot(feats, projection, preferred_element_type=jnp.float32).astype(jnp.bfloat16)
    neighbour = projected[:, :out_width].reshape(devices, BLK_DEV, tile_size, out_width)
    self_part = projected[:, out_width:]
    tile_sets = tiles.reshape(devices, SLOTS_DEV, KB, tile_size, tile_size)
    sources = source_block.reshape(devices, SLOTS_DEV, KB)
    device_ids = jnp.arange(devices, dtype=jnp.int32)
    dest_device = slot_owner.reshape(devices, SLOTS_DEV) * N_FEAT + (device_ids % N_FEAT)[:, None]
    destination = (dest_device * BLK_DEV + slot_block.reshape(devices, SLOTS_DEV)).astype(jnp.int32)

    def accumulate(running, inputs):
        tile_set, source, blocks_here, target = inputs
        picked = blocks_here[source]
        contribution = jnp.einsum('skij,skjh->sih', tile_set.astype(jnp.float32), picked.astype(jnp.float32)).astype(jnp.bfloat16)
        return running.at[target].add(contribution.astype(jnp.float32)), None

    start_sum = jnp.zeros((devices * BLK_DEV, tile_size, out_width), jnp.float32)
    summed, unused = lax.scan(accumulate, start_sum, (tile_sets, sources, neighbour, destination))
    summed = summed.reshape(-1, out_width)
    degree = counts.astype(jnp.float32)[:, None]
    preact = summed / degree + self_part.astype(jnp.float32)
    sigma = jax.nn.sigmoid(preact)
    activated = (preact * sigma).astype(jnp.bfloat16)
    grad_pre = out_grad.astype(jnp.float32) * sigma * (1.0 + preact * (1.0 - sigma))
    grad_self = grad_pre.astype(jnp.bfloat16)
    grad_sum = (grad_pre / degree).astype(jnp.bfloat16)
    grad_blocks = grad_sum.reshape(devices * BLK_DEV, tile_size, out_width)

    def backward(inputs):
        tile_set, source, target = inputs
        slot_grad = grad_blocks[target]
        products = jnp.einsum('skij,sih->skjh', tile_set.astype(jnp.float32), slot_grad.astype(jnp.float32))
        source_hot = (jnp.arange(BLK_DEV, dtype=jnp.int32)[:, None] == source.reshape(-1)[None, :]).astype(jnp.float32)
        flat_products = products.reshape(SLOTS_DEV * KB, tile_size, out_width)
        return jnp.einsum('bn,njh->bjh', source_hot, flat_products, precision=lax.Precision.HIGHEST).astype(jnp.bfloat16)

    grad_neigh = lax.map(backward, (tile_sets, sources, destination)).reshape(-1, out_width)
    grad_proj = jnp.concatenate([grad_neigh, grad_self], axis=1)
    weight_grad = lax.dot_general(feats, grad_proj, (((0,), (0,)), ((), ())), preferred_element_type=jnp.float32)
    return activated, weight_grad
```

```python
import functools

import jax
import jax.numpy as jnp
from jax import lax
from jax.experimental import pallas as pl
from jax.experimental.pallas import tpu as pltpu
from jax.sharding import PartitionSpec as P


BF16 = jnp.bfloat16
F32 = jnp.float32


def xor_pairs(count, offset):
    return [(i, i ^ offset) for i in range(count)]


def dot(a, b):
    return jnp.dot(a, b, preferred_element_type=F32)


def slots_kernel(parts, per_slot, step_slots, half, index_ref, source_ref, *refs):
    pieces, weights = refs[:parts], refs[parts : 2 * parts]
    tiles_ref, far_ref, near_ref, blocks, acc = refs[2 * parts :]
    step = pl.program_id(0)
    size = tiles_ref.shape[-1]

    @pl.when(step == 0)
    def start():
        projected = dot(pieces[0][...], weights[0][...])
        for piece, weight in zip(pieces[1:], weights[1:]):
            projected = projected + dot(piece[...], weight[...])
        projected = projected.astype(BF16)
        for b in range(blocks.shape[0]):
            blocks[b] = projected[b * size : (b + 1) * size]
        acc[...] = jnp.zeros_like(acc)

    def one(s, carry):
        slot = step * step_slots + s
        left = jnp.concatenate([tiles_ref[s, k] for k in range(per_slot)], axis=1)
        right = jnp.concatenate(
            [blocks[source_ref[slot * per_slot + k]] for k in range(per_slot)], axis=0
        )
        value = dot(left, right).astype(BF16).astype(F32)
        where = index_ref[slot]
        acc[where] = acc[where] + value
        return carry

    lax.fori_loop(0, step_slots, one, 0)

    @pl.when(step == pl.num_programs(0) - 1)
    def finish():
        far_ref[...] = acc[half:].astype(BF16)
        near_ref[...] = acc[:half]


def whole(shape):
    return pl.BlockSpec(shape, lambda *_: (0,) * len(shape))


def slot_sums(index, source, pieces, weights, tiles, dest_count):
    slots, per_slot, size, _ = tiles.shape
    width = weights[0].shape[1]
    block_count = pieces[0].shape[0] // size
    step_slots = min(slots, 8)
    half = dest_count // 2
    tile_spec = pl.BlockSpec(
        (step_slots, per_slot, size, size), lambda i, *_: (i, 0, 0, 0)
    )
    return pl.pallas_call(
        functools.partial(slots_kernel, len(pieces), per_slot, step_slots, half),
        out_shape=(
            jax.ShapeDtypeStruct((half, size, width), BF16),
            jax.ShapeDtypeStruct((half, size, width), F32),
        ),
        grid_spec=pltpu.PrefetchScalarGridSpec(
            num_scalar_prefetch=2,
            grid=(slots // step_slots,),
            in_specs=[whole(p.shape) for p in pieces]
            + [whole(w.shape) for w in weights]
            + [tile_spec],
            out_specs=(whole((half, size, width)), whole((half, size, width))),
            scratch_shapes=[
                pltpu.VMEM((block_count, size, width), BF16),
                pltpu.VMEM((dest_count, size, width), F32),
            ],
        ),
        name="slot_sums",
    )(index, source, *pieces, *weights, tiles)


def self_kernel(parts, *refs):
    pieces, weights, out = refs[:parts], refs[parts : 2 * parts], refs[2 * parts]
    total = dot(pieces[0][...], weights[0][...])
    for piece, weight in zip(pieces[1:], weights[1:]):
        total = total + dot(piece[...], weight[...])
    out[...] = total.astype(BF16)


def self_product(pieces, weights):
    return pl.pallas_call(
        functools.partial(self_kernel, len(pieces)),
        out_shape=jax.ShapeDtypeStruct(
            (pieces[0].shape[0], weights[0].shape[1]), BF16
        ),
        name="self_product",
    )(*pieces, *weights)


def node_kernel(count, *refs):
    got = refs[:count]
    own, counts, out_grad, active, sum_t, self_t = refs[count:]
    size = got[0].shape[1]
    for b in range(got[0].shape[0]):
        rows = pl.ds(b * size, size)
        summed = got[0][b].astype(F32)
        for other in got[1:]:
            summed = summed + other[b].astype(F32)
        degree = counts[rows, :].astype(F32)
        preact = summed / degree + own[rows, :].astype(F32)
        sigma = jax.nn.sigmoid(preact)
        active[rows, :] = (preact * sigma).astype(BF16)
        grad = out_grad[rows, :].astype(F32) * sigma * (1.0 + preact * (1.0 - sigma))
        self_t[:, rows] = grad.astype(BF16).T
        sum_t[b] = (grad / degree).astype(BF16).T


def node_step(got, own, counts, out_grad):
    blocks, size, width = got[0].shape
    rows = blocks * size
    return pl.pallas_call(
        functools.partial(node_kernel, len(got)),
        out_shape=(
            jax.ShapeDtypeStruct((rows, width), BF16),
            jax.ShapeDtypeStruct((blocks, width, size), BF16),
            jax.ShapeDtypeStruct((width, rows), BF16),
        ),
        name="node_step",
    )(*got, own, counts, out_grad)


def weight_kernel(parts, *refs):
    grad, pieces, outs = refs[0], refs[1 : 1 + parts], refs[1 + parts :]
    for piece, out in zip(pieces, outs):
        out[...] = dot(grad[...], piece[...]).astype(BF16)


def weight_product(grad, pieces):
    shape = jax.ShapeDtypeStruct((grad.shape[0], pieces[0].shape[1]), BF16)
    return pl.pallas_call(
        functools.partial(weight_kernel, len(pieces)),
        out_shape=(shape,) * len(pieces),
        name="self_weight",
    )(grad, *pieces)


def back_kernel(count, parts, per_slot, step_slots, index_ref, source_ref, *refs):
    grads, pieces = refs[:count], refs[count : count + parts]
    tiles_ref = refs[count + parts]
    outs = refs[count + parts + 1 : count + 2 * parts + 1]
    table, acc = refs[count + 2 * parts + 1 :]
    step = pl.program_id(0)
    size = tiles_ref.shape[-1]

    @pl.when(step == 0)
    def start():
        blocks = grads[0].shape[0]
        for g, grad in enumerate(grads):
            table[g * blocks : (g + 1) * blocks] = grad[...]
        acc[...] = jnp.zeros_like(acc)

    def one(s, carry):
        slot = step * step_slots + s
        right = jnp.concatenate([tiles_ref[s, k] for k in range(per_slot)], axis=1)
        value = dot(table[index_ref[slot]], right)
        for k in range(per_slot):
            where = source_ref[slot * per_slot + k]
            acc[where] = acc[where] + value[:, k * size : (k + 1) * size]
        return carry

    lax.fori_loop(0, step_slots, one, 0)

    @pl.when(step == pl.num_programs(0) - 1)
    def finish():
        grad = jnp.concatenate([acc[b].astype(BF16) for b in range(acc.shape[0])], axis=1)
        for piece, out in zip(pieces, outs):
            out[...] = dot(grad, piece[...]).astype(BF16)


def back_step(index, source, grads, pieces, tiles):
    slots, per_slot, size, _ = tiles.shape
    blocks, width, _ = grads[0].shape
    block_count = pieces[0].shape[0] // size
    step_slots = min(slots, 8)
    out = jax.ShapeDtypeStruct((width, pieces[0].shape[1]), BF16)
    tile_spec = pl.BlockSpec(
        (step_slots, per_slot, size, size), lambda i, *_: (i, 0, 0, 0)
    )
    return pl.pallas_call(
        functools.partial(back_kernel, len(grads), len(pieces), per_slot, step_slots),
        out_shape=(out,) * len(pieces),
        grid_spec=pltpu.PrefetchScalarGridSpec(
            num_scalar_prefetch=2,
            grid=(slots // step_slots,),
            in_specs=[whole(g.shape) for g in grads]
            + [whole(p.shape) for p in pieces]
            + [tile_spec],
            out_specs=(whole(out.shape),) * len(pieces),
            scratch_shapes=[
                pltpu.VMEM((len(grads) * blocks, width, size), BF16),
                pltpu.VMEM((block_count, width, size), F32),
            ],
        ),
        name="back_step",
    )(index, source, *grads, *pieces, tiles)


def final_kernel(near_ref, near_got, self_ref, self_got, out_ref):
    width = near_ref.shape[0]
    near = near_ref[...].astype(F32) + near_got[...].astype(F32)
    out_ref[:, :width] = near.T
    own = self_ref[...].astype(F32) + self_got[...].astype(F32)
    out_ref[:, width:] = own.T


def final_step(near, near_got, own, own_got):
    width, columns = near.shape
    return pl.pallas_call(
        final_kernel,
        out_shape=jax.ShapeDtypeStruct((columns, 2 * width), F32),
        name="final_step",
    )(near, near_got, own, own_got)


def local(feats, projection, tiles, slot_owner, slot_block, source_block, counts, out_grad):
    size = tiles.shape[-1]
    width = out_grad.shape[1]
    rows = out_grad.shape[0]
    blocks = rows // size
    nf = lax.axis_size("feat")
    nd = lax.axis_size("dom")
    nz = nd // 2
    fi = lax.axis_index("feat")
    di = lax.axis_index("dom")

    def over_feat(x, k):
        return lax.ppermute(x, "feat", xor_pairs(nf, k))

    def over_dom(x, k):
        return lax.ppermute(x, "dom", xor_pairs(nd, k))

    def weights_of(part):
        even = [part] + [over_feat(part, k) for k in range(2, nf, 2)]
        odd = [over_feat(w, 1) for w in even]
        return [w for pair in zip(even, odd) for w in pair]

    cut = feats.reshape(nf, rows, feats.shape[1])
    pieces = [lax.dynamic_index_in_dim(cut, fi ^ k, 0, keepdims=False) for k in range(nf)]
    pieces = [pieces[0]] + [over_feat(pieces[k], k) for k in range(1, nf)]
    near_weights = weights_of(projection[:, :width])
    self_weights = weights_of(projection[:, width:])

    relative = slot_owner[:, 0] ^ di
    index_c = ((relative % 2) * nz + relative // 2) * blocks + slot_block[:, 0]
    source = source_block.reshape(-1)

    far, near = slot_sums(index_c, source, pieces, near_weights, tiles, nd * blocks)
    got = over_dom(far, 1)
    both = [
        (
            near[z * blocks : (z + 1) * blocks] + got[z * blocks : (z + 1) * blocks].astype(F32)
        ).astype(BF16)
        for z in range(nz)
    ]
    arrived = [both[0]] + [over_dom(both[z], 2 * z) for z in range(1, nz)]
    own = self_product(pieces, self_weights)
    activated, sum_t, self_t = node_step(arrived, own, counts[:, None], out_grad)

    by_z = [sum_t] + [over_dom(sum_t, 2 * z) for z in range(1, nz)]
    by_y = [over_dom(g, 1) for g in by_z]

    self_parts = weight_product(self_t, pieces)

    def feat_sum(parts):
        total = parts[0].astype(F32)
        for k in range(1, nf):
            total = total + over_feat(parts[k], k).astype(F32)
        return total.astype(BF16)

    def dom_sum(x):
        k = 1
        while 2 * k < nd:
            x = (x.astype(F32) + over_dom(x, k).astype(F32)).astype(BF16)
            k *= 2
        return x, over_dom(x, k)

    self_sum = dom_sum(feat_sum(self_parts))
    near_parts = back_step(index_c, source, by_z + by_y, pieces, tiles)
    near_sum = dom_sum(feat_sum(near_parts))
    weight_grad = final_step(*near_sum, *self_sum)
    return activated, weight_grad


def solution(mesh):
    placed = (
        P("dom", "feat"),
        P("feat", None),
        P(("dom", "feat"), None, None, None),
        P(("dom", "feat"), None),
        P(("dom", "feat"), None),
        P(("dom", "feat"), None),
        P(("dom", "feat")),
        P(("dom", "feat"), None),
    )
    return jax.shard_map(
        local,
        mesh=mesh,
        in_specs=placed,
        out_specs=(P(("dom", "feat"), None), P("feat", None)),
        check_vma=False,
    )
```

```python
import functools

import jax
import jax.numpy as jnp
from jax import lax
from jax.experimental import pallas as pl
from jax.experimental.pallas import tpu as pltpu
from jax.sharding import PartitionSpec as P


BF16 = jnp.bfloat16
F32 = jnp.float32


def xor_pairs(count, offset):
    return [(i, i ^ offset) for i in range(count)]


def dot(a, b):
    return jnp.dot(a, b, preferred_element_type=F32)


def slots_kernel(parts, per_slot, step_slots, group, half, chunks, index_ref, source_ref, *refs):
    pieces, weights = refs[:parts], refs[parts : 2 * parts]
    tiles_ref, outs = refs[2 * parts], refs[2 * parts + 1 : -2]
    blocks, acc = refs[-2:]
    step = pl.program_id(0)
    size = tiles_ref.shape[-1]

    @pl.when(step == 0)
    def start():
        projected = dot(pieces[0][...], weights[0][...])
        for piece, weight in zip(pieces[1:], weights[1:]):
            projected = projected + dot(piece[...], weight[...])
        projected = projected.astype(BF16)
        for b in range(blocks.shape[0]):
            blocks[b] = projected[b * size : (b + 1) * size]
        acc[...] = jnp.zeros_like(acc)

    def some(g, carry):
        values = []
        for u in range(group):
            s = g * group + u
            slot = step * step_slots + s
            left = jnp.concatenate([tiles_ref[s, k] for k in range(per_slot)], axis=1)
            right = jnp.concatenate(
                [blocks[source_ref[slot * per_slot + k]] for k in range(per_slot)], axis=0
            )
            values.append((index_ref[slot], dot(left, right).astype(BF16).astype(F32)))
        for where, value in values:
            acc[where] = acc[where] + value
        return carry

    lax.fori_loop(0, step_slots // group, some, 0)

    @pl.when(step == pl.num_programs(0) - 1)
    def finish():
        for c, (first, count) in enumerate(chunks):
            far, near = outs[2 * c : 2 * c + 2]
            for z in range(half // blocks.shape[0]):
                at = z * blocks.shape[0] + first
                far[z * count : (z + 1) * count] = acc[half + at : half + at + count].astype(BF16)
                near[z * count : (z + 1) * count] = acc[at : at + count]


def whole(shape):
    return pl.BlockSpec(shape, lambda *_: (0,) * len(shape))


def slot_sums(index, source, pieces, weights, tiles, dest_count, chunks):
    slots, per_slot, size, _ = tiles.shape
    width = weights[0].shape[1]
    block_count = pieces[0].shape[0] // size
    step_slots, group = min(slots, 16), min(slots, 8)
    half = dest_count // 2
    shapes = []
    for _, count in chunks:
        shape = (half // block_count * count, size, width)
        shapes += [jax.ShapeDtypeStruct(shape, BF16), jax.ShapeDtypeStruct(shape, F32)]
    tile_spec = pl.BlockSpec(
        (step_slots, per_slot, size, size), lambda i, *_: (i, 0, 0, 0)
    )
    return pl.pallas_call(
        functools.partial(
            slots_kernel, len(pieces), per_slot, step_slots, group, half, chunks
        ),
        out_shape=tuple(shapes),
        grid_spec=pltpu.PrefetchScalarGridSpec(
            num_scalar_prefetch=2,
            grid=(slots // step_slots,),
            in_specs=[whole(p.shape) for p in pieces]
            + [whole(w.shape) for w in weights]
            + [tile_spec],
            out_specs=tuple(whole(shape.shape) for shape in shapes),
            scratch_shapes=[
                pltpu.VMEM((block_count, size, width), BF16),
                pltpu.VMEM((dest_count, size, width), F32),
            ],
        ),
        name="slot_sums",
    )(index, source, *pieces, *weights, tiles)


def self_kernel(parts, *refs):
    pieces, weights, out = refs[:parts], refs[parts : 2 * parts], refs[2 * parts]
    total = dot(pieces[0][...], weights[0][...])
    for piece, weight in zip(pieces[1:], weights[1:]):
        total = total + dot(piece[...], weight[...])
    out[...] = total.astype(BF16)


def self_product(pieces, weights):
    return pl.pallas_call(
        functools.partial(self_kernel, len(pieces)),
        out_shape=jax.ShapeDtypeStruct(
            (pieces[0].shape[0], weights[0].shape[1]), BF16
        ),
        name="self_product",
    )(*pieces, *weights)


def node_kernel(count, first, *refs):
    got = refs[:count]
    own, counts, out_grad, active, sum_t, self_t = refs[count:]
    size = got[0].shape[1]
    for b in range(got[0].shape[0]):
        rows, source = pl.ds(b * size, size), pl.ds((first + b) * size, size)
        summed = got[0][b].astype(F32)
        for other in got[1:]:
            summed = summed + other[b].astype(F32)
        degree = counts[source, :].astype(F32)
        preact = summed / degree + own[source, :].astype(F32)
        sigma = jax.nn.sigmoid(preact)
        active[rows, :] = (preact * sigma).astype(BF16)
        grad = out_grad[source, :].astype(F32) * sigma * (1.0 + preact * (1.0 - sigma))
        self_t[:, rows] = grad.astype(BF16).T
        sum_t[b] = (grad / degree).astype(BF16).T


def node_step(first, got, own, counts, out_grad):
    blocks, size, width = got[0].shape
    rows = blocks * size
    return pl.pallas_call(
        functools.partial(node_kernel, len(got), first),
        out_shape=(
            jax.ShapeDtypeStruct((rows, width), BF16),
            jax.ShapeDtypeStruct((blocks, width, size), BF16),
            jax.ShapeDtypeStruct((width, rows), BF16),
        ),
        name="node_step",
    )(*got, own, counts, out_grad)


def weight_kernel(count, parts, *refs):
    grads, pieces, outs = refs[:count], refs[count : count + parts], refs[count + parts :]
    grad = jnp.concatenate([g[...] for g in grads], axis=1)
    for piece, out in zip(pieces, outs):
        out[...] = dot(grad, piece[...]).astype(BF16)


def weight_product(grads, pieces):
    shape = jax.ShapeDtypeStruct((grads[0].shape[0], pieces[0].shape[1]), BF16)
    return pl.pallas_call(
        functools.partial(weight_kernel, len(grads), len(pieces)),
        out_shape=(shape,) * len(pieces),
        name="self_weight",
    )(*grads, *pieces)


def back_kernel(count, parts, per_slot, step_slots, group, places, index_ref, source_ref, *refs):
    grads, pieces = refs[:count], refs[count : count + parts]
    tiles_ref = refs[count + parts]
    outs = refs[count + parts + 1 : count + 2 * parts + 1]
    table, acc = refs[count + 2 * parts + 1 :]
    step = pl.program_id(0)
    size = tiles_ref.shape[-1]

    @pl.when(step == 0)
    def start():
        for place, grad in zip(places, grads):
            table[place : place + grad.shape[0]] = grad[...]
        acc[...] = jnp.zeros_like(acc)

    def some(g, carry):
        values = []
        for u in range(group):
            s = g * group + u
            slot = step * step_slots + s
            right = jnp.concatenate([tiles_ref[s, k] for k in range(per_slot)], axis=1)
            values.append((slot, dot(table[index_ref[slot]], right)))
        for slot, value in values:
            for k in range(per_slot):
                where = source_ref[slot * per_slot + k]
                acc[where] = acc[where] + value[:, k * size : (k + 1) * size]
        return carry

    lax.fori_loop(0, step_slots // group, some, 0)

    @pl.when(step == pl.num_programs(0) - 1)
    def finish():
        grad = jnp.concatenate([acc[b].astype(BF16) for b in range(acc.shape[0])], axis=1)
        for piece, out in zip(pieces, outs):
            out[...] = dot(grad, piece[...]).astype(BF16)


def back_step(index, source, places, grads, pieces, tiles):
    slots, per_slot, size, _ = tiles.shape
    _, width, _ = grads[0].shape
    block_count = pieces[0].shape[0] // size
    step_slots, group = min(slots, 16), min(slots, 8)
    out = jax.ShapeDtypeStruct((width, pieces[0].shape[1]), BF16)
    tile_spec = pl.BlockSpec(
        (step_slots, per_slot, size, size), lambda i, *_: (i, 0, 0, 0)
    )
    return pl.pallas_call(
        functools.partial(
            back_kernel, len(grads), len(pieces), per_slot, step_slots, group, places
        ),
        out_shape=(out,) * len(pieces),
        grid_spec=pltpu.PrefetchScalarGridSpec(
            num_scalar_prefetch=2,
            grid=(slots // step_slots,),
            in_specs=[whole(g.shape) for g in grads]
            + [whole(p.shape) for p in pieces]
            + [tile_spec],
            out_specs=(whole(out.shape),) * len(pieces),
            scratch_shapes=[
                pltpu.VMEM((sum(g.shape[0] for g in grads), width, size), BF16),
                pltpu.VMEM((block_count, width, size), F32),
            ],
        ),
        name="back_step",
    )(index, source, *grads, *pieces, tiles)


def final_kernel(near_ref, near_got, self_ref, self_got, out_ref):
    width = near_ref.shape[0]
    near = near_ref[...].astype(F32) + near_got[...].astype(F32)
    out_ref[:, :width] = near.T
    own = self_ref[...].astype(F32) + self_got[...].astype(F32)
    out_ref[:, width:] = own.T


def final_step(near, near_got, own, own_got):
    width, columns = near.shape
    return pl.pallas_call(
        final_kernel,
        out_shape=jax.ShapeDtypeStruct((columns, 2 * width), F32),
        name="final_step",
    )(near, near_got, own, own_got)


def local(feats, projection, tiles, slot_owner, slot_block, source_block, counts, out_grad):
    size = tiles.shape[-1]
    width = out_grad.shape[1]
    rows = out_grad.shape[0]
    blocks = rows // size
    nf = lax.axis_size("feat")
    nd = lax.axis_size("dom")
    nz = nd // 2
    fi = lax.axis_index("feat")
    di = lax.axis_index("dom")

    def over_feat(x, k):
        return lax.ppermute(x, "feat", xor_pairs(nf, k))

    def over_dom(x, k):
        return lax.ppermute(x, "dom", xor_pairs(nd, k))

    def weights_of(part):
        even = [part] + [over_feat(part, k) for k in range(2, nf, 2)]
        odd = [over_feat(w, 1) for w in even]
        return [w for pair in zip(even, odd) for w in pair]

    cut = feats.reshape(nf, rows, feats.shape[1])
    pieces = [lax.dynamic_index_in_dim(cut, fi ^ k, 0, keepdims=False) for k in range(nf)]
    pieces = [pieces[0]] + [over_feat(pieces[k], k) for k in range(1, nf)]
    near_weights = weights_of(projection[:, :width])
    self_weights = weights_of(projection[:, width:])

    relative = slot_owner[:, 0] ^ di
    index_c = ((relative % 2) * nz + relative // 2) * blocks + slot_block[:, 0]
    source = source_block.reshape(-1)

    middle = blocks // 2
    chunks = ((0, middle), (middle, blocks - middle))
    sums = slot_sums(index_c, source, pieces, near_weights, tiles, nd * blocks, chunks)
    own = self_product(pieces, self_weights)
    degrees = counts[:, None]

    got = None
    active, self_t, places, grads = [], [], [], []
    for c, (first, count) in enumerate(chunks):
        far, near = sums[2 * c : 2 * c + 2]
        if got is not None:
            far, got = lax.optimization_barrier((far, got))
        got = over_dom(far, 1)
        both = [
            (
                near[z * count : (z + 1) * count]
                + got[z * count : (z + 1) * count].astype(F32)
            ).astype(BF16)
            for z in range(nz)
        ]
        arrived = [both[0]] + [over_dom(both[z], 2 * z) for z in range(1, nz)]
        out, sum_t, grad_t = node_step(first, arrived, own, degrees, out_grad)
        active.append(out)
        self_t.append(grad_t)
        by_z = [sum_t] + [over_dom(sum_t, 2 * z) for z in range(1, nz)]
        by_y = [over_dom(g, 1) for g in by_z]
        grads += by_z + by_y
        places += [r * blocks + first for r in range(nd)]
    activated = jnp.concatenate(active, axis=0)
    self_parts = weight_product(self_t, pieces)

    def feat_sum(parts):
        total = parts[0].astype(F32)
        for k in range(1, nf):
            total = total + over_feat(parts[k], k).astype(F32)
        return total.astype(BF16)

    def dom_sum(x):
        k = 1
        while 2 * k < nd:
            x = (x.astype(F32) + over_dom(x, k).astype(F32)).astype(BF16)
            k *= 2
        return x, over_dom(x, k)

    self_sum = dom_sum(feat_sum(self_parts))
    near_parts = back_step(index_c, source, tuple(places), grads, pieces, tiles)
    near_sum = dom_sum(feat_sum(near_parts))
    weight_grad = final_step(*near_sum, *self_sum)
    return activated, weight_grad


def solution(mesh):
    placed = (
        P("dom", "feat"),
        P("feat", None),
        P(("dom", "feat"), None, None, None),
        P(("dom", "feat"), None),
        P(("dom", "feat"), None),
        P(("dom", "feat"), None),
        P(("dom", "feat")),
        P(("dom", "feat"), None),
    )
    return jax.shard_map(
        local,
        mesh=mesh,
        in_specs=placed,
        out_specs=(P(("dom", "feat"), None), P("feat", None)),
        check_vma=False,
    )
```

```python
import functools

import jax
import jax.numpy as jnp
from jax import lax
from jax.experimental import pallas as pl
from jax.experimental.pallas import tpu as pltpu
from jax.sharding import PartitionSpec as P


BF16 = jnp.bfloat16
F32 = jnp.float32


def xor_pairs(count, offset):
    return [(i, i ^ offset) for i in range(count)]


def vmem(mib):
    return pltpu.CompilerParams(vmem_limit_bytes=mib * 1024 * 1024)


def gate(x, after):
    return lax.optimization_barrier((x, after))[0]


def dot(a, b):
    return jnp.dot(a, b, preferred_element_type=F32)


def slots_kernel(parts, per_slot, step_slots, group, half, chunks, index_ref, source_ref, *refs):
    pieces, weights = refs[:parts], refs[parts : 2 * parts]
    tiles_ref, outs = refs[2 * parts], refs[2 * parts + 1 : -2]
    blocks, acc = refs[-2:]
    step = pl.program_id(0)
    size = tiles_ref.shape[-1]

    @pl.when(step == 0)
    def start():
        projected = dot(pieces[0][...], weights[0][...])
        for piece, weight in zip(pieces[1:], weights[1:]):
            projected = projected + dot(piece[...], weight[...])
        projected = projected.astype(BF16)
        for b in range(blocks.shape[0]):
            blocks[b] = projected[b * size : (b + 1) * size]
        acc[...] = jnp.zeros_like(acc)

    def some(g, carry):
        values = []
        for u in range(group):
            s = g * group + u
            slot = step * step_slots + s
            left = jnp.concatenate([tiles_ref[s, k] for k in range(per_slot)], axis=1)
            right = jnp.concatenate(
                [blocks[source_ref[slot * per_slot + k]] for k in range(per_slot)], axis=0
            )
            values.append((index_ref[slot], dot(left, right).astype(BF16).astype(F32)))
        for where, value in values:
            acc[where] = acc[where] + value
        return carry

    lax.fori_loop(0, step_slots // group, some, 0)

    @pl.when(step == pl.num_programs(0) - 1)
    def finish():
        for c, (first, count) in enumerate(chunks):
            far, near = outs[2 * c : 2 * c + 2]
            for z in range(half // blocks.shape[0]):
                at = z * blocks.shape[0] + first
                far[z * count : (z + 1) * count] = acc[half + at : half + at + count].astype(BF16)
                near[z * count : (z + 1) * count] = acc[at : at + count]


def whole(shape):
    return pl.BlockSpec(shape, lambda *_: (0,) * len(shape))


def slot_sums(index, source, pieces, weights, tiles, dest_count, chunks):
    slots, per_slot, size, _ = tiles.shape
    width = weights[0].shape[1]
    block_count = pieces[0].shape[0] // size
    step_slots, group = min(slots, 16), min(slots, 8)
    half = dest_count // 2
    shapes = []
    for _, count in chunks:
        shape = (half // block_count * count, size, width)
        shapes += [jax.ShapeDtypeStruct(shape, BF16), jax.ShapeDtypeStruct(shape, F32)]
    tile_spec = pl.BlockSpec(
        (step_slots, per_slot, size, size), lambda i, *_: (i, 0, 0, 0)
    )
    return pl.pallas_call(
        functools.partial(
            slots_kernel, len(pieces), per_slot, step_slots, group, half, chunks
        ),
        out_shape=tuple(shapes),
        grid_spec=pltpu.PrefetchScalarGridSpec(
            num_scalar_prefetch=2,
            grid=(slots // step_slots,),
            in_specs=[whole(p.shape) for p in pieces]
            + [whole(w.shape) for w in weights]
            + [tile_spec],
            out_specs=tuple(whole(shape.shape) for shape in shapes),
            scratch_shapes=[
                pltpu.VMEM((block_count, size, width), BF16),
                pltpu.VMEM((dest_count, size, width), F32),
            ],
        ),
        compiler_params=vmem(20),
        name="slot_sums",
    )(index, source, *pieces, *weights, tiles)


def self_kernel(parts, *refs):
    pieces, weights, out = refs[:parts], refs[parts : 2 * parts], refs[2 * parts]
    total = dot(pieces[0][...], weights[0][...])
    for piece, weight in zip(pieces[1:], weights[1:]):
        total = total + dot(piece[...], weight[...])
    out[...] = total.astype(BF16)


def self_product(pieces, weights):
    return pl.pallas_call(
        functools.partial(self_kernel, len(pieces)),
        out_shape=jax.ShapeDtypeStruct(
            (pieces[0].shape[0], weights[0].shape[1]), BF16
        ),
        compiler_params=vmem(6),
        name="self_product",
    )(*pieces, *weights)


def node_kernel(count, first, *refs):
    got = refs[:count]
    own, counts, out_grad, active, sum_t, self_t = refs[count:]
    size = got[0].shape[1]
    for b in range(got[0].shape[0]):
        rows, source = pl.ds(b * size, size), pl.ds((first + b) * size, size)
        summed = got[0][b].astype(F32)
        for other in got[1:]:
            summed = summed + other[b].astype(F32)
        degree = counts[first + b : first + b + 1, :].astype(F32)
        degree = jnp.broadcast_to(degree, (size, size)).T
        degree = jnp.concatenate([degree] * (out_grad.shape[1] // size), axis=1)
        preact = summed / degree + own[source, :].astype(F32)
        sigma = jax.nn.sigmoid(preact)
        active[rows, :] = (preact * sigma).astype(BF16)
        grad = out_grad[source, :].astype(F32) * sigma * (1.0 + preact * (1.0 - sigma))
        self_t[:, rows] = grad.astype(BF16).T
        sum_t[b] = (grad / degree).astype(BF16).T


def node_step(first, got, own, counts, out_grad):
    blocks, size, width = got[0].shape
    rows = blocks * size
    return pl.pallas_call(
        functools.partial(node_kernel, len(got), first),
        out_shape=(
            jax.ShapeDtypeStruct((rows, width), BF16),
            jax.ShapeDtypeStruct((blocks, width, size), BF16),
            jax.ShapeDtypeStruct((width, rows), BF16),
        ),
        compiler_params=vmem(6),
        name="node_step",
    )(*got, own, counts, out_grad)


def weight_kernel(count, parts, *refs):
    grads, pieces, outs = refs[:count], refs[count : count + parts], refs[count + parts :]
    grad = jnp.concatenate([g[...] for g in grads], axis=1)
    for piece, out in zip(pieces, outs):
        out[...] = dot(grad, piece[...]).astype(BF16)


def weight_product(grads, pieces):
    shape = jax.ShapeDtypeStruct((grads[0].shape[0], pieces[0].shape[1]), BF16)
    return pl.pallas_call(
        functools.partial(weight_kernel, len(grads), len(pieces)),
        out_shape=(shape,) * len(pieces),
        compiler_params=vmem(6),
        name="self_weight",
    )(*grads, *pieces)


def back_kernel(count, parts, per_slot, step_slots, group, places, index_ref, source_ref, *refs):
    grads, pieces = refs[:count], refs[count : count + parts]
    tiles_ref = refs[count + parts]
    outs = refs[count + parts + 1 : count + 2 * parts + 1]
    table, acc = refs[count + 2 * parts + 1 :]
    step = pl.program_id(0)
    size = tiles_ref.shape[-1]

    @pl.when(step == 0)
    def start():
        for place, grad in zip(places, grads):
            table[place : place + grad.shape[0]] = grad[...]
        acc[...] = jnp.zeros_like(acc)

    def some(g, carry):
        values = []
        for u in range(group):
            s = g * group + u
            slot = step * step_slots + s
            right = jnp.concatenate([tiles_ref[s, k] for k in range(per_slot)], axis=1)
            values.append((slot, dot(table[index_ref[slot]], right)))
        for slot, value in values:
            for k in range(per_slot):
                where = source_ref[slot * per_slot + k]
                acc[where] = acc[where] + value[:, k * size : (k + 1) * size]
        return carry

    lax.fori_loop(0, step_slots // group, some, 0)

    @pl.when(step == pl.num_programs(0) - 1)
    def finish():
        grad = jnp.concatenate([acc[b].astype(BF16) for b in range(acc.shape[0])], axis=1)
        for piece, out in zip(pieces, outs):
            out[...] = dot(grad, piece[...]).astype(BF16)


def back_step(index, source, places, grads, pieces, tiles):
    slots, per_slot, size, _ = tiles.shape
    _, width, _ = grads[0].shape
    block_count = pieces[0].shape[0] // size
    step_slots, group = min(slots, 16), min(slots, 8)
    out = jax.ShapeDtypeStruct((width, pieces[0].shape[1]), BF16)
    tile_spec = pl.BlockSpec(
        (step_slots, per_slot, size, size), lambda i, *_: (i, 0, 0, 0)
    )
    return pl.pallas_call(
        functools.partial(
            back_kernel, len(grads), len(pieces), per_slot, step_slots, group, places
        ),
        out_shape=(out,) * len(pieces),
        grid_spec=pltpu.PrefetchScalarGridSpec(
            num_scalar_prefetch=2,
            grid=(slots // step_slots,),
            in_specs=[whole(g.shape) for g in grads]
            + [whole(p.shape) for p in pieces]
            + [tile_spec],
            out_specs=(whole(out.shape),) * len(pieces),
            scratch_shapes=[
                pltpu.VMEM((sum(g.shape[0] for g in grads), width, size), BF16),
                pltpu.VMEM((block_count, width, size), F32),
            ],
        ),
        compiler_params=vmem(20),
        name="back_step",
    )(index, source, *grads, *pieces, tiles)


def final_kernel(near_ref, near_got, self_ref, self_got, out_ref):
    width = near_ref.shape[0]
    near = near_ref[...].astype(F32) + near_got[...].astype(F32)
    out_ref[:, :width] = near.T
    own = self_ref[...].astype(F32) + self_got[...].astype(F32)
    out_ref[:, width:] = own.T


def final_step(near, near_got, own, own_got):
    width, columns = near.shape
    return pl.pallas_call(
        final_kernel,
        out_shape=jax.ShapeDtypeStruct((columns, 2 * width), F32),
        compiler_params=vmem(6),
        name="final_step",
    )(near, near_got, own, own_got)


def local(feats, projection, tiles, slot_owner, slot_block, source_block, counts, out_grad):
    size = tiles.shape[-1]
    width = out_grad.shape[1]
    rows = out_grad.shape[0]
    blocks = rows // size
    nf = lax.axis_size("feat")
    nd = lax.axis_size("dom")
    nz = nd // 2
    fi = lax.axis_index("feat")
    di = lax.axis_index("dom")

    def over_feat(x, k):
        return lax.ppermute(x, "feat", xor_pairs(nf, k))

    def over_dom(x, k):
        return lax.ppermute(x, "dom", xor_pairs(nd, k))

    def weights_of(part):
        even = [part] + [over_feat(part, k) for k in range(2, nf, 2)]
        odd = [over_feat(w, 1) for w in even]
        return [w for pair in zip(even, odd) for w in pair]

    cut = feats.reshape(nf, rows, feats.shape[1])
    pieces = [lax.dynamic_index_in_dim(cut, fi ^ k, 0, keepdims=False) for k in range(nf)]
    pieces = [pieces[0]] + [over_feat(pieces[k], k) for k in range(1, nf)]
    near_weights = weights_of(projection[:, :width])

    relative = slot_owner[:, 0] ^ di
    index_c = ((relative % 2) * nz + relative // 2) * blocks + slot_block[:, 0]
    source = source_block.reshape(-1)

    middle = blocks // 2
    chunks = ((0, middle), (middle, blocks - middle))
    sums = slot_sums(index_c, source, pieces, near_weights, tiles, nd * blocks, chunks)
    own_part = gate(projection[:, width:], sums[0])
    self_weights = [own_part] + [over_feat(own_part, k) for k in range(1, nf)]
    own = self_product(pieces, self_weights)
    degrees = counts.reshape(blocks, size)

    got = None
    active, self_t, places, grads = [], [], [], []
    for c, (first, count) in enumerate(chunks):
        far, near = sums[2 * c : 2 * c + 2]
        if got is not None:
            far, got = lax.optimization_barrier((far, got))
        got = over_dom(far, 1)
        both = [
            (
                near[z * count : (z + 1) * count]
                + got[z * count : (z + 1) * count].astype(F32)
            ).astype(BF16)
            for z in range(nz)
        ]
        arrived = [both[0]] + [over_dom(both[z], 2 * z) for z in range(1, nz)]
        out, sum_t, grad_t = node_step(first, arrived, own, degrees, out_grad)
        active.append(out)
        self_t.append(grad_t)
        by_z = [sum_t] + [over_dom(sum_t, 2 * z) for z in range(1, nz)]
        by_y = [over_dom(g, 1) for g in by_z]
        grads += by_z + by_y
        places += [r * blocks + first for r in range(nd)]
    activated = jnp.concatenate(active, axis=0)
    self_parts = weight_product(self_t, pieces)

    def feat_sum(parts):
        total = parts[0].astype(F32)
        for k in range(1, nf):
            total = total + over_feat(parts[k], k).astype(F32)
        return total.astype(BF16)

    def dom_sum(x, steps):
        for k in steps[:-1]:
            x = (x.astype(F32) + over_dom(x, k).astype(F32)).astype(BF16)
        return x, over_dom(x, steps[-1])

    steps = [1]
    while 2 * steps[-1] < nd:
        steps.append(2 * steps[-1])
    self_sum = dom_sum(gate(feat_sum(self_parts), by_z[-1]), steps[1:] + steps[:1])
    near_parts = back_step(index_c, source, tuple(places), grads, pieces, tiles)
    near_sum = dom_sum(feat_sum(near_parts), steps)
    weight_grad = final_step(*near_sum, *self_sum)
    return activated, weight_grad


def solution(mesh):
    placed = (
        P("dom", "feat"),
        P("feat", None),
        P(("dom", "feat"), None, None, None),
        P(("dom", "feat"), None),
        P(("dom", "feat"), None),
        P(("dom", "feat"), None),
        P(("dom", "feat")),
        P(("dom", "feat"), None),
    )
    return jax.shard_map(
        local,
        mesh=mesh,
        in_specs=placed,
        out_specs=(P(("dom", "feat"), None), P("feat", None)),
        check_vma=False,
    )
```
